256 devices in a mesh: gx: 16 (over y, x), gy: 16 (over z, core).
Axes of the slice: x: 4, y: 4, z: 8, core: 2. Of those that a mesh axis runs over, the one named last changes fastest.
Arguments:
- volume: float32 [512, 1024, 256], P('gx', 'gy'), may hold values from -18 to 18, as said below
Outputs:
- denoised: float32 [512, 1024, 256], P('gx', 'gy')
The draws below stay inside these ranges and needn't reach their ends.
Inputs may be any that keep to these rules, and one draw needn't show every extreme that they name: `volume`: real values.
All inputs are finite; a program needn't handle non-finite values.
Results may differ from the reference program's by a relative error of at most 0.00002.
Values sent between devices are 32-bit elements; how exact they have to be, the bound alone decides.
No kernel may reach another device: no remote copies, remote signals or barrier semaphores. Data moves between devices by JAX's collectives and lax.ppermute only.
A program may use at most 128 MiB of HBM per device.

```python
import math
import jax
import jax.numpy as jnp

NZ = 256
LEVELS = 3
NX = 512
NY = 1024


def draw_volume(key, part):
    ramp_x = 1.0 + 2.0 * jnp.arange(NX, dtype=jnp.float32)[:, None, None] / NX
    noise = jnp.clip(jax.random.normal(key, (NX, NY, NZ), jnp.float32), -6.0, 6.0)
    return (ramp_x * noise).astype(jnp.float32)


def setup_inputs(seed: int = 0) -> dict:
    seeds = jax.random.split(jax.random.key(seed), 2)
    return {
        "volume": draw_volume(jax.random.fold_in(seeds[1], 71), 0),
    }


root_three = math.sqrt(3.0)
lift_near = math.sqrt(3.0) / 4.0
lift_far = (math.sqrt(3.0) - 2.0) / 4.0
scale_low = (math.sqrt(3.0) - 1.0) / math.sqrt(2.0)
scale_high = (math.sqrt(3.0) + 1.0) / math.sqrt(2.0)

def take_every(values, start, along):
    index = [slice(None)] * values.ndim
    index[along] = slice(start, None, 2)
    return values[tuple(index)]

def weave(first, second, along):
    stacked = jnp.stack([first, second], axis=along + 1)
    shape = list(first.shape)
    shape[along] = shape[along] * 2
    return stacked.reshape(shape)

def forward_lines(values, along):
    even_cells = take_every(values, 0, along)
    odd_cells = take_every(values, 1, along)
    smooth = even_cells + root_three * odd_cells
    detail = odd_cells - lift_near * smooth - lift_far * jnp.roll(smooth, 1, axis=along)
    smooth = smooth - jnp.roll(detail, -1, axis=along)
    return (scale_high * detail, scale_low * smooth)

def inverse_lines(detail, smooth, along):
    detail = detail / scale_high
    smooth = smooth / scale_low
    first = smooth + jnp.roll(detail, -1, axis=along)
    odd_cells = detail + lift_near * first + lift_far * jnp.roll(first, 1, axis=along)
    even_cells = first - root_three * odd_cells
    return weave(even_cells, odd_cells, along)

def forward_level(coarse):
    detail, smooth = forward_lines(coarse, 0)
    coeffs = weave(detail, smooth, 0)
    detail, smooth = forward_lines(coeffs, 1)
    coeffs = weave(detail, smooth, 1)
    detail, smooth = forward_lines(coeffs, 2)
    return jnp.concatenate([smooth, detail], axis=2)

def inverse_level(coeffs):
    half = coeffs.shape[2] // 2
    rebuilt = inverse_lines(coeffs[:, :, half:], coeffs[:, :, :half], 2)
    rebuilt = inverse_lines(take_every(rebuilt, 0, 1), take_every(rebuilt, 1, 1), 1)
    return inverse_lines(take_every(rebuilt, 0, 0), take_every(rebuilt, 1, 0), 0)

def split_view(coeffs):
    sizes = coeffs.shape
    return coeffs.reshape(sizes[0] // 2, 2, sizes[1] // 2, 2, sizes[2])

def shrink_insert(coeffs, coarse, limit):
    shrunk = coeffs - jnp.clip(coeffs, -limit, limit)
    half = coeffs.shape[2] // 2
    view = split_view(shrunk).at[:, 1, :, 1, :half].set(coarse)
    return view.reshape(coeffs.shape)

def reference(volume):
    levels = []
    coarse = volume
    for level in range(LEVELS):
        coeffs = forward_level(coarse)
        levels.append(coeffs)
        half = coeffs.shape[2] // 2
        coarse = split_view(coeffs)[:, 1, :, 1, :half]
    finest = levels[0]
    half = finest.shape[2] // 2
    diagonal = split_view(finest)[:, 0, :, 0, half:]
    count = NX * NY * NZ // 8
    noise = jnp.sum(jnp.abs(diagonal)) * (math.sqrt(math.pi / 2.0) / count)
    rebuilt = coarse
    for level in range(LEVELS - 1, -1, -1):
        coeffs = shrink_insert(levels[level], rebuilt, noise)
        rebuilt = inverse_level(coeffs)
    return rebuilt
```

```python
import math

import jax
import jax.numpy as jnp
import numpy as np
from jax import lax
from jax.experimental import pallas as pl
from jax.experimental.pallas import tpu as pltpu
from jax.sharding import PartitionSpec as P

R3 = math.sqrt(3.0)
NEAR = R3 / 4.0
FAR = (R3 - 2.0) / 4.0
K0 = (R3 - 1.0) / math.sqrt(2.0)
K1 = (R3 + 1.0) / math.sqrt(2.0)
DD, SS = K1 * K1, K0 * K0
F32 = jnp.float32
BF16 = jnp.bfloat16
VMEM = pl.BlockSpec(memory_space=pltpu.VMEM)


def depth_matrix(n):
    v = np.eye(n)
    e, o = v[:, 0::2], v[:, 1::2]
    s = e + R3 * o
    d = o - NEAR * s - FAR * np.roll(s, 1, axis=1)
    s = s - np.roll(d, -1, axis=1)
    return np.concatenate([K0 * s, K1 * d], axis=1)


def halves(m):
    m = np.asarray(m, np.float32)
    hi = m.astype(BF16)
    lo = (m - hi.astype(np.float32)).astype(BF16)
    return jnp.asarray(hi), jnp.asarray(lo)


def times(x, hi_ref, lo_ref):
    hi = x.astype(BF16)
    lo = (x - hi.astype(F32)).astype(BF16)
    w, v = hi_ref[...], lo_ref[...]
    dot = lambda p, q: jnp.dot(p, q, preferred_element_type=F32)
    return dot(hi, w) + (dot(lo, w) + dot(hi, v))


def lift_x(load, store, pairs):
    o = load(1)
    s0 = load(0) + R3 * o
    o = load(3)
    s1 = load(2) + R3 * o
    d1 = o - NEAR * s1 - FAR * s0
    for m in range(1, pairs - 1):
        o = load(2 * m + 3)
        s2 = load(2 * m + 2) + R3 * o
        d2 = o - NEAR * s2 - FAR * s1
        store(m - 1, 0, d1)
        store(m - 1, 1, s1 - d2)
        s1, d1 = s2, d2


def lift_y(load):
    s0 = load(0) + R3 * load(1)
    o1 = load(3)
    s1 = load(2) + R3 * o1
    o2 = load(5)
    s2 = load(4) + R3 * o2
    d1 = o1 - NEAR * s1 - FAR * s0
    d2 = o2 - NEAR * s2 - FAR * s1
    return d1, s1 - d2


def unlift(d0, d1, sm, s0):
    first = s0 + d1
    o = d0 + NEAR * first + FAR * (sm + d0)
    return first - R3 * o, o


def unlift_x(load, store, pairs):
    d1 = load(1, 0)
    before = load(0, 1) + d1
    for m in range(1, pairs - 1):
        d2 = load(m + 1, 0)
        first = load(m, 1) + d2
        o = d1 + NEAR * first + FAR * before
        store(2 * m - 2, first - R3 * o)
        store(2 * m - 1, o)
        d1, before = d2, first


def shrink(c, t):
    return c - jnp.clip(c, -t, t)


def forward_one(vol, hx, hy, wh, wl, c1, cc1, m2x, ex, ey, ext, zin):
    @pl.loop(0, 4)
    def _(c):
        rows = pl.ds(pl.multiple_of(c * 16, 16), 16)

        def load(k):
            return vol[k, rows, :] if k < 32 else hx[k - 32, rows, :]

        def store(i, p, v):
            ext[i, p, 0, rows, :] = v[:, :128]
            ext[i, p, 1, rows, :] = v[:, 128:]

        lift_x(load, store, 18)

    def put(i, p, v):
        ext[i, p, 0, 64:68, :] = v[:, :128]
        ext[i, p, 1, 64:68, :] = v[:, 128:]

    lift_x(lambda k: hy[k], put, 18)

    def group(g, acc):
        for q in range(4):
            for p in range(2):
                i = g * 4 + q
                base = (q * 2 + p) * 64
                for h in range(2):
                    d, s = lift_y(lambda k: ext[i, p, h, pl.ds(k, 32, stride=2), :])
                    lanes = slice(h * 128, h * 128 + 128)
                    zin[base : base + 32, lanes] = d
                    zin[base + 32 : base + 64, lanes] = s
        u = times(zin[...], wh, wl).reshape(4, 2, 2, 32, 256)
        c1[pl.ds(g * 4, 4)] = u
        cc1[pl.ds(g * 4, 4)] = u[:, 1, 1, :, :128]
        return acc + jnp.sum(jnp.abs(u[:, 0, 0, :, 128:]).reshape(16, 8, 128), axis=0)

    acc = lax.fori_loop(0, 4, group, jnp.zeros((8, 128), F32))
    m2x[0:13] = cc1[0:13]
    m2x[13] = jnp.full((32, 128), jnp.sum(acc), F32)
    ex[0] = c1[14, 1]
    ex[1] = c1[15, 0]
    ex[2] = c1[15, 1]
    for i in range(16):
        for p in range(2):
            ey[2 * i + p, 0:1, :] = c1[i, p, 1, 30:31, :]
            ey[2 * i + p, 1:2, :] = c1[i, p, 0, 31:32, :]
            ey[2 * i + p, 2:3, :] = c1[i, p, 1, 31:32, :]
            ey[2 * i + p, 3:4, :] = c1[i, p, 1, 31:32, :]


def pack_two(cc1, m2x, r2x, m2y):
    m2y[0:15] = cc1[1:16, 0:16]
    m2y[15:28] = r2x[0:13, 0:16]
    m2y[28] = m2x[13, 0:16] + r2x[13, 0:16]


def forward_rest(
    cc1, r2x, r2y, ex, w2h, w2l, w3h, w3l, c2, c3, m3x, x2, z2, x3, z3
):
    def near(k):
        return cc1[k + 1] if k < 15 else r2x[k - 15]

    def put_near(i, p, v):
        x2[i, p, 0:32, :] = v

    def put_far(i, p, v):
        x2[i, p, 32:48, :] = v
        x2[i, p, 48:56, :] = jnp.zeros((8, 128), F32)

    lift_x(near, put_near, 14)
    lift_x(lambda k: r2y[k], put_far, 14)
    for i in range(12):
        for p in range(2):
            d, s = lift_y(lambda k: x2[i, p, pl.ds(k + 1, 24, stride=2), :])
            base = (i * 2 + p) * 48
            z2[base : base + 24, :] = d
            z2[base + 24 : base + 48, :] = s
    c2[...] = times(z2[...], w2h, w2l).reshape(12, 2, 2, 24, 128)

    def put3(i, p, v):
        x3[i, p, :, :] = v

    lift_x(lambda k: c2[k, 1, 1], put3, 6)
    for i in range(4):
        for p in range(2):
            d, s = lift_y(lambda k: x3[i, p, pl.ds(k, 8, stride=2), :])
            base = (i * 2 + p) * 16
            z3[base : base + 8, :] = d
            z3[base + 8 : base + 16, :] = s
    u = times(z3[...], w3h, w3l)
    c3[...] = u.reshape(4, 2, 2, 8, 128)
    m3x[0:128, :] = u
    m3x[128:384, :] = c2[4:8, :, :, 0:16, :].reshape(256, 128)
    e = ex[...].reshape(192, 256)
    m3x[384:576, :] = e[:, :128]
    m3x[576:768, :] = e[:, 128:]


def left_one(r3x, k):
    lo = r3x[384 + 64 * k : 448 + 64 * k, :]
    hi = r3x[576 + 64 * k : 640 + 64 * k, :]
    return jnp.concatenate([lo, hi], axis=1).reshape(2, 32, 256)


def pack_three(c2, c3, ey, r3x, m3y):
    for i in range(8):
        for p in range(2):
            for q in range(2):
                at = ((i * 2 + p) * 2 + q) * 4
                if i < 4:
                    src = ((i * 2 + p) * 2 + q) * 8 + 4
                    m3y[at : at + 4, :] = r3x[src : src + 4, :]
                else:
                    m3y[at : at + 4, :] = c3[i - 4, p, q, 4:8, :]
    for i in range(12):
        for p in range(2):
            for q in range(2):
                at = 128 + ((i * 2 + p) * 2 + q) * 4
                if i < 4:
                    src = 128 + ((i * 2 + p) * 2 + q) * 16 + 12
                    m3y[at : at + 4, :] = r3x[src : src + 4, :]
                else:
                    m3y[at : at + 4, :] = c2[i - 4, p, q, 12:16, :]
    for k in range(34):
        at = 320 + k * 4
        if k < 3:
            for h in range(2):
                src = 384 + 192 * h + 64 * k
                to = at + 136 * h
                m3y[to : to + 1, :] = r3x[src + 62 : src + 63, :]
                m3y[to + 1 : to + 2, :] = r3x[src + 31 : src + 32, :]
                m3y[to + 2 : to + 3, :] = r3x[src + 63 : src + 64, :]
                m3y[to + 3 : to + 4, :] = r3x[src + 63 : src + 64, :]
        else:
            m3y[at : at + 4, :] = ey[k - 3, :, 0:128]
            m3y[at + 136 : at + 140, :] = ey[k - 3, :, 128:256]


def inverse_all(
    c1, c2, c3, r3x, r3y, ta, tb, w1h, w1l, w2h, w2l, w3h, w3l, out,
    u3, y3, z3, u2, y2, z2, dd, ss, y1, z1, *, factor
):
    noise = (ta[0:1, :] + tb[0:1, :]) * factor
    wide = jnp.concatenate([noise, noise], axis=1)
    scale = {(0, 0): 1.0 / DD, (0, 1): 1.0, (1, 0): 1.0, (1, 1): DD}

    for i in range(8):
        for p in range(2):
            for q in range(2):
                t = noise * (scale[p, q] * DD * DD)
                n = (i * 2 + p) * 2 + q
                if i < 4:
                    mid = r3x[n * 8 : n * 8 + 8, :]
                else:
                    mid = c3[i - 4, p, q]
                top = r3y[n * 4 : n * 4 + 4, :]
                u3[i, p, q, 4:8, :] = shrink(top, t)
                if p and q:
                    low = lax.broadcasted_iota(jnp.int32, (8, 128), 1) < 32
                    u3[i, p, q, 8:16, :] = jnp.where(low, mid, shrink(mid, t))
                    low = low[0:4]
                    u3[i, p, q, 4:8, :] = jnp.where(low, top, shrink(top, t))
                else:
                    u3[i, p, q, 8:16, :] = shrink(mid, t)
            e, o = unlift(
                u3[i, p, 0, 5:15, :],
                u3[i, p, 0, 6:16, :],
                u3[i, p, 1, 4:14, :],
                u3[i, p, 1, 5:15, :],
            )
            y3[i, p, 0:4, :] = jnp.zeros((4, 128), F32)
            y3[i, p, pl.ds(4, 10, stride=2), :] = e
            y3[i, p, pl.ds(5, 10, stride=2), :] = o

    def put3(k, v):
        z3[k * 24 : k * 24 + 24, :] = v

    unlift_x(lambda m, p: y3[m, p], put3, 8)
    rb2 = times(z3[...], w3h, w3l).reshape(12, 24, 128)

    for i in range(12):
        for p in range(2):
            for q in range(2):
                t = noise * (scale[p, q] * DD)
                n = (i * 2 + p) * 2 + q
                if i < 4:
                    mid = r3x[128 + n * 16 : 144 + n * 16, :]
                else:
                    mid = c2[i - 4, p, q, 0:16, :]
                u2[i, p, q, 4:8, :] = shrink(r3y[128 + n * 4 : 132 + n * 4, :], t)
                u2[i, p, q, 8:24, :] = shrink(mid, t)
            if p:
                u2[i, 1, 1, :, 0:64] = rb2[i][:, 0:64]
            e, o = unlift(
                u2[i, p, 0, 5:23, :],
                u2[i, p, 0, 6:24, :],
                u2[i, p, 1, 4:22, :],
                u2[i, p, 1, 5:23, :],
            )
            y2[i, p, 0:8, :] = jnp.zeros((8, 128), F32)
            y2[i, p, 40:48, :] = jnp.zeros((8, 128), F32)
            y2[i, p, pl.ds(5, 18, stride=2), :] = e
            y2[i, p, pl.ds(6, 18, stride=2), :] = o

    def put2(k, v):
        z2[k * 48 : k * 48 + 48, :] = v

    unlift_x(lambda m, p: y2[m, p], put2, 12)
    z2[...] = times(z2[...], w2h, w2l)

    t_d = {p: wide * scale[p, 0] for p in range(2)}
    t_s = {p: wide * scale[p, 1] for p in range(2)}

    def layer(l, p, mid_d, mid_s, cell):
        lo, hi = r3y[pl.ds(320 + l * 4, 4), :], r3y[pl.ds(456 + l * 4, 4), :]
        top = jnp.concatenate([lo, hi], axis=1)
        dd[p, 7:8, :] = shrink(top[1:2], t_d[p])
        dd[p, 8:40, :] = shrink(mid_d, t_d[p])
        ss[p, 6:7, :] = shrink(top[0:1], t_s[p])
        ss[p, 7:8, :] = shrink(top[2:3], t_s[p])
        ss[p, 8:40, :] = shrink(mid_s, t_s[p])
        if p:
            ss[p, :, 0:128] = z2[pl.ds(cell * 48, 40), :]
        e, o = unlift(
            dd[p, 7:39, :], dd[p, 8:40, :], ss[p, 6:38, :], ss[p, 7:39, :]
        )
        for h in range(2):
            y1[l, h, pl.ds(0, 32, stride=2), :] = e[:, h * 128 : h * 128 + 128]
            y1[l, h, pl.ds(1, 32, stride=2), :] = o[:, h * 128 : h * 128 + 128]

    for k in range(3):
        mid = left_one(r3x, k)
        layer(k, 1 - k % 2, mid[0], mid[1], (k - 2) // 2 + 2)

    @pl.loop(0, 15)
    def _(i):
        layer(2 * i + 3, 0, c1[i, 0, 0], c1[i, 0, 1], None)
        layer(2 * i + 4, 1, c1[i, 1, 0], c1[i, 1, 1], i + 3)

    layer(33, 0, c1[15, 0, 0], c1[15, 0, 1], None)

    @pl.loop(0, 4)
    def _(c):
        rows = pl.ds(pl.multiple_of(c * 16, 16), 16)

        for h in range(2):

            def load(m, p):
                return y1[2 * m - 1 + p, h, rows, :]

            def put(k, v):
                z1[k, rows, h * 128 : h * 128 + 128] = v

            unlift_x(load, put, 18)

    @pl.loop(0, 4)
    def _(g):
        u = times(z1[pl.ds(g * 8, 8)].reshape(512, 256), w1h, w1l)
        out[pl.ds(g * 8, 8)] = u.reshape(8, 64, 256)


def call(body, outs, scratch, args, vmem_mib):
    return pl.pallas_call(
        body,
        out_shape=[jax.ShapeDtypeStruct(s, F32) for s in outs],
        in_specs=[VMEM] * len(args),
        out_specs=[VMEM] * len(outs),
        scratch_shapes=[pltpu.VMEM(s, F32) for s in scratch],
        compiler_params=pltpu.CompilerParams(vmem_limit_bytes=vmem_mib << 20),
    )(*args)


def from_ahead(v, axis, by):
    n = lax.axis_size(axis)
    return lax.ppermute(v, axis, [((i + by) % n, i) for i in range(n)])


def from_behind(v, axis):
    n = lax.axis_size(axis)
    return lax.ppermute(v, axis, [(i, (i + 1) % n) for i in range(n)])


def on_device(volume):
    w = {n: depth_matrix(n) for n in (256, 128, 64)}
    w[64] = np.pad(w[64], ((0, 64), (0, 64)))
    f1, f2, f3 = halves(w[256]), halves(w[128]), halves(w[64])
    b1, b2, b3 = halves(w[256].T), halves(w[128].T), halves(w[64].T)
    nx, ny = lax.axis_size("gx"), lax.axis_size("gy")

    hx = from_ahead(volume[0:4], "gx", 1)
    hy = from_ahead(
        jnp.concatenate([volume[:, 0:4], hx[:, 0:4]], axis=0), "gy", 1
    )
    c1, cc1, m2x, ex, ey = call(
        forward_one,
        [(16, 2, 2, 32, 256), (16, 32, 128), (14, 32, 128), (3, 2, 32, 256), (32, 4, 256)],
        [(16, 2, 2, 72, 128), (512, 256)],
        [volume, hx, hy, *f1],
        24,
    )
    r2x = from_ahead(m2x, "gx", 1)
    (m2y,) = call(pack_two, [(29, 16, 128)], [], [cc1, m2x, r2x], 8)
    r2y = from_ahead(m2y, "gy", 1)
    total = m2y[28, 0:8] + r2y[28, 0:8]
    steps = [(a, 1 << k) for a, n in (("gx", nx), ("gy", ny)) for k in range(1, 8) if 1 << k < n]
    other = jnp.zeros_like(total)
    for k, (axis, by) in enumerate(steps):
        other = from_ahead(total, axis, by)
        if k < len(steps) - 1:
            total = total + other

    c2, c3, m3x = call(
        forward_rest,
        [(12, 2, 2, 24, 128), (4, 2, 2, 8, 128), (768, 128)],
        [(12, 2, 56, 128), (1152, 128), (4, 2, 24, 128), (128, 128)],
        [cc1, r2x, r2y, ex, *f2, *f3],
        12,
    )
    r3x = from_behind(m3x, "gx")
    (m3y,) = call(pack_three, [(592, 128)], [], [c2, c3, ey, r3x], 8)
    r3y = from_behind(m3y, "gy")
    count = nx * ny * volume.size // 8
    factor = math.sqrt(math.pi / 2.0) / count * DD

    def body(*refs):
        inverse_all(*refs, factor=factor)

    (out,) = call(
        body,
        [volume.shape],
        [
            (8, 2, 2, 16, 128), (8, 2, 24, 128), (288, 128),
            (12, 2, 2, 24, 128), (12, 2, 48, 128), (960, 128),
            (2, 40, 256), (2, 40, 256), (34, 2, 64, 128), (32, 64, 256),
        ],
        [c1, c2, c3, r3x, r3y, total, other, *b1, *b2, *b3],
        24,
    )
    return out


def solution(mesh):
    return jax.shard_map(
        on_device,
        mesh=mesh,
        in_specs=(P("gx", "gy", None),),
        out_specs=P("gx", "gy", None),
        check_vma=False,
    )
```

```python
import math

import jax
import jax.numpy as jnp
from jax import lax
from jax.experimental import pallas as pl
from jax.experimental.pallas import tpu as pltpu
from jax.sharding import PartitionSpec as P

R3 = math.sqrt(3.0)
NEAR = R3 / 4.0
FAR = (R3 - 2.0) / 4.0
K0 = (R3 - 1.0) / math.sqrt(2.0)
K1 = (R3 + 1.0) / math.sqrt(2.0)
DD = K1 * K1
F32 = jnp.float32
BF16 = jnp.bfloat16
VMEM = pl.BlockSpec(memory_space=pltpu.VMEM)
HBM = pl.BlockSpec(memory_space=pltpu.HBM)


def depth_weights(n, hi_ref, lo_ref):
    shape = hi_ref.shape
    cell = lax.broadcasted_iota(jnp.int32, shape, 0)
    place = lax.broadcasted_iota(jnp.int32, shape, 1)
    at = (cell - 2 * place) & (n - 1)
    low = {0: 1 + FAR, 1: R3 * (1 + FAR), 2: NEAR, 3: NEAR * R3 - 1}
    high = {0: -NEAR, 1: 1 - NEAR * R3, n - 2: -FAR, n - 1: -FAR * R3}
    w = jnp.zeros(shape, F32)
    for k, v in low.items():
        w = jnp.where((at == k) & (place < n // 2), K0 * v, w)
    for k, v in high.items():
        w = jnp.where((at == k) & (place >= n // 2), K1 * v, w)
    if shape[0] > n:
        w = jnp.where((cell < n) & (place < n), w, 0.0)
    hi = w.astype(BF16)
    hi_ref[...] = hi
    lo_ref[...] = (w - hi.astype(F32)).astype(BF16)


def times(x, hi_ref, lo_ref, back=False):
    hi = x.astype(BF16)
    lo = (x - hi.astype(F32)).astype(BF16)
    w, v = hi_ref[...], lo_ref[...]
    dims = (((1,), (1 if back else 0,)), ((), ()))
    dot = lambda p, q: lax.dot_general(p, q, dims, preferred_element_type=F32)
    return dot(hi, w) + (dot(lo, w) + dot(hi, v))


def raw(cell):
    def pair(m):
        o = cell(2 * m + 1)
        s = cell(2 * m) + R3 * o
        return s, o - NEAR * s

    return pair


def lift_x(pair, store, pairs):
    s0, _ = pair(0)
    s1, q1 = pair(1)
    d1 = q1 - FAR * s0
    for m in range(1, pairs - 1):
        s2, q2 = pair(m + 1)
        d2 = q2 - FAR * s1
        store(m - 1, 0, d1)
        store(m - 1, 1, s1 - d2)
        s1, d1 = s2, d2


def lift_y(load):
    s0 = load(0) + R3 * load(1)
    o1 = load(3)
    s1 = load(2) + R3 * o1
    o2 = load(5)
    s2 = load(4) + R3 * o2
    d1 = o1 - NEAR * s1 - FAR * s0
    d2 = o2 - NEAR * s2 - FAR * s1
    return d1, s1 - d2


def unlift(d0, d1, sm, s0):
    first = s0 + d1
    o = d0 + NEAR * first + FAR * (sm + d0)
    return first - R3 * o, o


def unlift_x(load, store, pairs):
    d1 = load(1, 0)
    before = load(0, 1) + d1
    for m in range(1, pairs - 1):
        d2 = load(m + 1, 0)
        first = load(m, 1) + d2
        o = d1 + NEAR * first + FAR * before
        store(2 * m - 2, first - R3 * o)
        store(2 * m - 1, o)
        d1, before = d2, first


def shrink(c, t):
    return c - jnp.clip(c, -t, t)


def depth_one(vol, zc, wh, wl):
    depth_weights(256, wh, wl)

    @pl.loop(0, 4)
    def _(g):
        u = times(vol[pl.ds(g * 8, 8)].reshape(512, 256), wh, wl)
        zc[pl.ds(g * 8, 8)] = u.reshape(8, 64, 256)


def forward_one(
    zc, hx, hy, hd, c1, cc1, ahead, behind, part, ey, ext, hxz, hyz, wh, wl
):
    depth_weights(256, wh, wl)
    for k in range(35):
        hyz[4 * k : 4 * k + 4, :] = hy[k] if k < 32 else hd[k - 32]
    hyz[140:144, :] = jnp.zeros((4, 256), F32)
    hxz[...] = times(hx[...].reshape(192, 256), wh, wl).reshape(3, 64, 256)
    hyz[...] = times(hyz[...], wh, wl)

    def spread(cell, edge):
        inner = raw(cell)

        def pair(m):
            if m < 16:
                return inner(m)
            return (edge(0), edge(1)) if m == 16 else (None, edge(2))

        return pair

    @pl.loop(0, 4)
    def _(c):
        rows = pl.ds(pl.multiple_of(c * 16, 16), 16)

        def store(i, p, v):
            ext[i, p, 0, rows, :] = v[:, :128]
            ext[i, p, 1, rows, :] = v[:, 128:]

        lift_x(spread(lambda k: zc[k, rows, :], lambda k: hxz[k, rows, :]), store, 18)

    def put(i, p, v):
        ext[i, p, 0, 64:68, :] = v[:, :128]
        ext[i, p, 1, 64:68, :] = v[:, 128:]

    def line(k):
        return hyz[4 * k : 4 * k + 4, :]

    lift_x(spread(line, lambda k: line(k + 32)), put, 18)

    def pair(i, acc):
        for p in range(2):
            for h in range(2):
                d, s = lift_y(lambda k: ext[i, p, h, pl.ds(k, 32, stride=2), :])
                lanes = slice(h * 128, h * 128 + 128)
                c1[i, p, 0, :, lanes] = d
                c1[i, p, 1, :, lanes] = s
                if (p, h) == (0, 1):
                    acc = acc + jnp.abs(d)
                if (p, h) == (1, 0):
                    cc1[i] = s
        return acc

    acc = lax.fori_loop(0, 16, pair, jnp.zeros((32, 128), F32))
    part[...] = jnp.full(part.shape, jnp.sum(acc), F32)
    ahead[...] = cc1[0:13]
    behind[0:480, :] = cc1[1:16].reshape(480, 128)
    for k, (i, p) in enumerate(((14, 1), (15, 0), (15, 1))):
        for q in range(2):
            for h in range(2):
                at = 480 + 192 * h + 64 * k + 32 * q
                behind[at : at + 32, :] = c1[i, p, q, :, h * 128 : h * 128 + 128]
    for i in range(16):
        for p in range(2):
            ey[2 * i + p, 0:1, :] = c1[i, p, 1, 30:31, :]
            ey[2 * i + p, 1:2, :] = c1[i, p, 0, 31:32, :]
            ey[2 * i + p, 2:3, :] = c1[i, p, 1, 31:32, :]
            ey[2 * i + p, 3:4, :] = c1[i, p, 1, 31:32, :]


def pack(cc1, r2r, r2l, ey, parts, ahead, behind, part):
    total = jnp.sum(parts[...], axis=0, keepdims=True)
    part[...] = jnp.broadcast_to(total, part.shape)
    for k in range(15):
        ahead[k] = r2l[32 * k : 32 * k + 16, :]
        behind[16 * k : 16 * k + 16, :] = r2l[32 * k + 16 : 32 * k + 32, :]
    for k in range(16):
        ahead[k + 15] = cc1[k, 0:16, :]
        behind[240 + 16 * k : 256 + 16 * k, :] = cc1[k, 16:32, :]
    for k in range(13):
        ahead[k + 31] = r2r[k, 0:16, :]
        behind[496 + 16 * k : 512 + 16 * k, :] = r2r[k, 16:32, :]
    for k in range(34):
        for h in range(2):
            to = 704 + k * 4 + 136 * h
            if k < 3:
                src = 480 + 192 * h + 64 * k
                behind[to : to + 1, :] = r2l[src + 62 : src + 63, :]
                behind[to + 1 : to + 2, :] = r2l[src + 31 : src + 32, :]
                behind[to + 2 : to + 3, :] = r2l[src + 63 : src + 64, :]
                behind[to + 3 : to + 4, :] = r2l[src + 63 : src + 64, :]
            else:
                behind[to : to + 4, :] = ey[k - 3, :, h * 128 : h * 128 + 128]


def forward_rest(
    cc1, r2r, r2l, r2u, r2d, parts, c2, c3, total, x2, z2, x3, z3, w2h, w2l, w3h, w3l
):
    depth_weights(128, w2h, w2l)
    depth_weights(64, w3h, w3l)
    total[...] = jnp.sum(parts[...], axis=0, keepdims=True)

    def near(k):
        if k < 15:
            return r2l[32 * k : 32 * k + 32, :]
        return cc1[k - 15] if k < 31 else r2r[k - 31]

    def put(lo, hi):
        def store(i, p, v):
            x2[i, p, lo:hi, :] = v

        return store

    lift_x(raw(lambda k: r2d[16 * k : 16 * k + 16, :]), put(0, 16), 22)
    lift_x(raw(near), put(16, 48), 22)
    lift_x(raw(lambda k: r2u[k]), put(48, 64), 22)

    @pl.loop(0, 20)
    def _(i):
        for p in range(2):
            x2[i, p, 64:72, :] = jnp.zeros((8, 128), F32)
            d, s = lift_y(lambda k: x2[i, p, pl.ds(k + 1, 32, stride=2), :])
            z2[i, p, 0] = d
            z2[i, p, 1] = s

    u = times(z2[...].reshape(2560, 128), w2h, w2l)
    c2[...] = u.reshape(20, 2, 2, 32, 128)

    def put3(i, p, v):
        x3[i, p, :, :] = v

    lift_x(raw(lambda k: c2[k, 1, 1]), put3, 10)
    for i in range(8):
        for p in range(2):
            d, s = lift_y(lambda k: x3[i, p, pl.ds(k, 12, stride=2), :])
            z3[i, p, 0, 0:4, :] = jnp.zeros((4, 128), F32)
            z3[i, p, 0, 4:16, :] = d
            z3[i, p, 1, 0:4, :] = jnp.zeros((4, 128), F32)
            z3[i, p, 1, 4:16, :] = s
    u = times(z3[...].reshape(512, 128), w3h, w3l)
    c3[...] = u.reshape(8, 2, 2, 16, 128)


def left_one(r2l, k):
    lo = r2l[480 + 64 * k : 544 + 64 * k, :]
    hi = r2l[672 + 64 * k : 736 + 64 * k, :]
    return jnp.concatenate([lo, hi], axis=1).reshape(2, 32, 256)


def inverse_all(
    c1, c2, c3, r2l, r2d, total, out,
    u3, y3, z3, u2, y2, z2, dd, ss, y1, z1, sent,
    w1h, w1l, w2h, w2l, w3h, w3l, *, factor
):
    depth_weights(256, w1h, w1l)
    depth_weights(128, w2h, w2l)
    depth_weights(64, w3h, w3l)
    noise = total[...] * factor
    wide = jnp.concatenate([noise, noise], axis=1)
    scale = {(0, 0): 1.0 / DD, (0, 1): 1.0, (1, 0): 1.0, (1, 1): DD}

    for i in range(8):
        for p in range(2):
            for q in range(2):
                t = noise * (scale[p, q] * DD * DD)
                c = c3[i, p, q]
                kept = shrink(c, t)
                if p and q:
                    low = lax.broadcasted_iota(jnp.int32, (16, 128), 1) < 32
                    kept = jnp.where(low, c, kept)
                u3[i, p, q] = kept
            e, o = unlift(
                u3[i, p, 0, 5:15, :],
                u3[i, p, 0, 6:16, :],
                u3[i, p, 1, 4:14, :],
                u3[i, p, 1, 5:15, :],
            )
            y3[i, p, 0:4, :] = jnp.zeros((4, 128), F32)
            y3[i, p, pl.ds(4, 10, stride=2), :] = e
            y3[i, p, pl.ds(5, 10, stride=2), :] = o

    def put3(k, v):
        z3[k * 24 : k * 24 + 24, :] = v

    unlift_x(lambda m, p: y3[m, p], put3, 8)
    rb2 = times(z3[...], w3h, w3l, True).reshape(12, 24, 128)

    for i in range(12):
        for p in range(2):
            for q in range(2):
                t = noise * (scale[p, q] * DD)
                u2[i, p, q] = shrink(c2[i + 4, p, q, 0:24, :], t)
            if p:
                u2[i, 1, 1, :, 0:64] = rb2[i][:, 0:64]
            e, o = unlift(
                u2[i, p, 0, 5:23, :],
                u2[i, p, 0, 6:24, :],
                u2[i, p, 1, 4:22, :],
                u2[i, p, 1, 5:23, :],
            )
            y2[i, p, 0:8, :] = jnp.zeros((8, 128), F32)
            y2[i, p, 40:48, :] = jnp.zeros((8, 128), F32)
            y2[i, p, pl.ds(5, 18, stride=2), :] = e
            y2[i, p, pl.ds(6, 18, stride=2), :] = o

    def put2(k, v):
        z2[k * 48 : k * 48 + 48, :] = v

    unlift_x(lambda m, p: y2[m, p], put2, 12)
    z2[...] = times(z2[...], w2h, w2l, True)

    t_d = {p: wide * scale[p, 0] for p in range(2)}
    t_s = {p: wide * scale[p, 1] for p in range(2)}

    def layer(l, p, mid_d, mid_s, cell):
        lo, hi = r2d[pl.ds(704 + l * 4, 4), :], r2d[pl.ds(840 + l * 4, 4), :]
        top = jnp.concatenate([lo, hi], axis=1)
        dd[p, 7:8, :] = shrink(top[1:2], t_d[p])
        dd[p, 8:40, :] = shrink(mid_d, t_d[p])
        ss[p, 6:7, :] = shrink(top[0:1], t_s[p])
        ss[p, 7:8, :] = shrink(top[2:3], t_s[p])
        ss[p, 8:40, :] = shrink(mid_s, t_s[p])
        if p:
            ss[p, :, 0:128] = z2[pl.ds(cell * 48, 40), :]
        e, o = unlift(
            dd[p, 7:39, :], dd[p, 8:40, :], ss[p, 6:38, :], ss[p, 7:39, :]
        )
        for h in range(2):
            y1[l, h, pl.ds(0, 32, stride=2), :] = e[:, h * 128 : h * 128 + 128]
            y1[l, h, pl.ds(1, 32, stride=2), :] = o[:, h * 128 : h * 128 + 128]

    for k in range(3):
        mid = left_one(r2l, k)
        layer(k, 1 - k % 2, mid[0], mid[1], (k - 2) // 2 + 2)

    @pl.loop(0, 15)
    def _(i):
        layer(2 * i + 3, 0, c1[i, 0, 0], c1[i, 0, 1], None)
        layer(2 * i + 4, 1, c1[i, 1, 0], c1[i, 1, 1], i + 3)

    layer(33, 0, c1[15, 0, 0], c1[15, 0, 1], None)

    @pl.loop(0, 4)
    def _(c):
        rows = pl.ds(pl.multiple_of(c * 16, 16), 16)

        for h in range(2):

            def load(m, p):
                return y1[2 * m - 1 + p, h, rows, :]

            def put(k, v):
                z1[k, rows, h * 128 : h * 128 + 128] = v

            unlift_x(load, put, 18)

    def send(g):
        rows = pl.ds(g * 8, 8)
        return pltpu.make_async_copy(z1.at[rows], out.at[rows], sent.at[g])

    @pl.loop(0, 4)
    def _(g):
        u = times(z1[pl.ds(g * 8, 8)].reshape(512, 256), w1h, w1l, True)
        z1[pl.ds(g * 8, 8)] = u.reshape(8, 64, 256)
        send(g).start()

    for g in range(4):
        send(g).wait()


def call(body, outs, scratch, args, mib, in_space=VMEM, out_space=VMEM):
    scratch = [pltpu.VMEM(s, F32) if isinstance(s, tuple) else s for s in scratch]
    return pl.pallas_call(
        body,
        out_shape=[jax.ShapeDtypeStruct(s, F32) for s in outs],
        in_specs=[in_space] * len(args),
        out_specs=[out_space] * len(outs),
        scratch_shapes=scratch,
        compiler_params=pltpu.CompilerParams(vmem_limit_bytes=mib << 20),
    )(*args)


def shared(v, axis):
    return lax.all_to_all(v, axis, 0, 0, tiled=True)


def from_ahead(v, axis):
    n = lax.axis_size(axis)
    return lax.ppermute(v, axis, [((i + 1) % n, i) for i in range(n)])


def from_behind(v, axis):
    n = lax.axis_size(axis)
    return lax.ppermute(v, axis, [(i, (i + 1) % n) for i in range(n)])


def from_corner(v):
    nx, ny = lax.axis_size("gx"), lax.axis_size("gy")
    route = [
        ((i + 1) % nx * ny + (j + 1) % ny, i * ny + j)
        for i in range(nx)
        for j in range(ny)
    ]
    return lax.ppermute(v, ("gx", "gy"), route)


def on_device(volume):
    nx, ny = lax.axis_size("gx"), lax.axis_size("gy")
    wide = [pltpu.VMEM((256, 256), BF16)] * 2
    slim = [pltpu.VMEM((128, 128), BF16)] * 2
    s, q = raw(lambda k: volume[k])(0)
    mx = jnp.stack([s, q, raw(lambda k: volume[k])(1)[1]])
    my = volume[:, 0:4]
    md = mx[:, 0:4]
    hd = from_corner(md)
    hx = from_ahead(mx, "gx")
    hy = from_ahead(my, "gy")
    (zc,) = call(depth_one, [volume.shape], wide, [volume], 8)
    c1, cc1, ahead, behind, part, ey = call(
        forward_one,
        [
            (16, 2, 2, 32, 256), (16, 32, 128), (13, 32, 128), (864, 128),
            (ny, 128), (32, 4, 256),
        ],
        [(16, 2, 2, 72, 128), (3, 64, 256), (144, 256), *wide],
        [zc, hx, hy, hd],
        16,
    )
    r2l = from_behind(behind, "gx")
    r2r = from_ahead(ahead, "gx")
    parts = shared(part, "gy")
    ahead, behind, part = call(
        pack,
        [(44, 16, 128), (976, 128), (nx, 128)],
        [],
        [cc1, r2r, r2l, ey, parts],
        4,
    )
    r2d = from_behind(behind, "gy")
    r2u = from_ahead(ahead, "gy")
    parts = shared(part, "gx")
    c2, c3, total = call(
        forward_rest,
        [(20, 2, 2, 32, 128), (8, 2, 2, 16, 128), (1, 128)],
        [(20, 2, 72, 128), (20, 2, 2, 32, 128), (8, 2, 32, 128), (8, 2, 2, 16, 128), *slim, *slim],
        [cc1, r2r, r2l, r2u, r2d, parts],
        10,
    )
    count = nx * ny * volume.size // 8
    factor = math.sqrt(math.pi / 2.0) / count * DD

    def body(*refs):
        inverse_all(*refs, factor=factor)

    (out,) = call(
        body,
        [volume.shape],
        [
            (8, 2, 2, 16, 128), (8, 2, 24, 128), (288, 128),
            (12, 2, 2, 24, 128), (12, 2, 48, 128), (960, 128),
            (2, 40, 256), (2, 40, 256), (34, 2, 64, 128), (32, 64, 256),
            pltpu.SemaphoreType.DMA((4,)), *wide, *slim, *slim,
        ],
        [c1, c2, c3, r2l, r2d, total],
        16,
        out_space=HBM,
    )
    return out


def solution(mesh):
    return jax.shard_map(
        on_device,
        mesh=mesh,
        in_specs=(P("gx", "gy", None),),
        out_specs=P("gx", "gy", None),
        check_vma=False,
    )
```

```python
import math

import jax
import jax.numpy as jnp
from jax import lax
from jax.experimental import pallas as pl
from jax.experimental.pallas import tpu as pltpu
from jax.sharding import PartitionSpec as P

R3 = math.sqrt(3.0)
NEAR = R3 / 4.0
FAR = (R3 - 2.0) / 4.0
K0 = (R3 - 1.0) / math.sqrt(2.0)
K1 = (R3 + 1.0) / math.sqrt(2.0)
DD = K1 * K1
F32 = jnp.float32
BF16 = jnp.bfloat16
VMEM = pl.BlockSpec(memory_space=pltpu.VMEM)
HBM = pl.BlockSpec(memory_space=pltpu.HBM)


def depth_weights(n, ref, back=False):
    size = ref.shape[0] // 3
    low = {0: 1 + FAR, 1: R3 * (1 + FAR), 2: NEAR, 3: NEAR * R3 - 1}
    high = {0: -NEAR, 1: 1 - NEAR * R3, n - 2: -FAR, n - 1: -FAR * R3}
    low = {k: K0 * v for k, v in low.items()}
    high = {k: K1 * v for k, v in high.items()}

    def block(shape, row, col, kinds):
        cell = row + lax.broadcasted_iota(jnp.int32, shape, 0)
        place = col + lax.broadcasted_iota(jnp.int32, shape, 1)
        if back:
            cell, place = place, cell
        at = (cell - 2 * place) & (n - 1)
        parts = []
        for kind in kinds:
            w = jnp.zeros(shape, F32)
            for k, v in kind.items():
                w = jnp.where(at == k, v, w)
            parts.append(w)
        w = parts[0]
        if len(parts) > 1:
            w = jnp.where(place < n // 2, w, parts[1])
        if size > n:
            w = jnp.where((cell < n) & (place < n), w, 0.0)
        return w

    def save(row, col, w):
        hi = w.astype(BF16)
        lo = (w - hi.astype(F32)).astype(BF16)
        rows, cols = w.shape
        for base, v in ((0, hi), (size, hi), (2 * size, lo)):
            ref[base + row : base + row + rows, col : col + cols] = v

    if n == 256:
        for half, kind in ((0, low), (128, high)):
            shape, at = ((128, 256), (half, 0)) if back else ((256, 128), (0, half))
            save(*at, block(shape, *at, (kind,)))
    else:
        save(0, 0, block((size, size), 0, 0, (low, high)))


def times(x, w_ref):
    hi = x.astype(BF16)
    lo = (x - hi.astype(F32)).astype(BF16)
    x = jnp.concatenate([hi, lo, hi], axis=1)
    return jnp.dot(x, w_ref[...], preferred_element_type=F32)


def raw(cell):
    def pair(m):
        o = cell(2 * m + 1)
        s = cell(2 * m) + R3 * o
        return s, o - NEAR * s

    return pair


def lift_x(pair, store, pairs):
    s0, _ = pair(0)
    s1, q1 = pair(1)
    d1 = q1 - FAR * s0
    for m in range(1, pairs - 1):
        s2, q2 = pair(m + 1)
        d2 = q2 - FAR * s1
        store(m - 1, 0, d1)
        store(m - 1, 1, s1 - d2)
        s1, d1 = s2, d2


def lift_y(load):
    s0 = load(0) + R3 * load(1)
    o1 = load(3)
    s1 = load(2) + R3 * o1
    o2 = load(5)
    s2 = load(4) + R3 * o2
    d1 = o1 - NEAR * s1 - FAR * s0
    d2 = o2 - NEAR * s2 - FAR * s1
    return d1, s1 - d2


def unlift(d0, first, before):
    o = d0 + NEAR * first + FAR * before
    return first - R3 * o, o


def unlift_rows(d, s):
    first = s + pltpu.roll(d, d.shape[0] - 1, 0)
    return unlift(d, first, pltpu.roll(first, 1, 0))


def unlift_x(load, store, pairs):
    d1 = load(1, 0)
    before = load(0, 1) + d1
    for m in range(1, pairs - 1):
        d2 = load(m + 1, 0)
        first = load(m, 1) + d2
        o = d1 + NEAR * first + FAR * before
        store(2 * m - 2, first - R3 * o)
        store(2 * m - 1, o)
        d1, before = d2, first


def shrink(c, t):
    return c - jnp.clip(c, -t, t)


def depth_one(vol, zc, wf, wb):
    depth_weights(256, wf)
    depth_weights(256, wb, True)

    for g in range(4):
        rows = slice(g * 8, g * 8 + 8)
        u = times(vol[rows].reshape(512, 256), wf)
        zc[rows] = u.reshape(8, 64, 256)


def forward_one(
    zc, hx, hy, hd, wf, c1, cc1, ahead, behind, part, ey, ext, hxz, hyz
):
    for k in range(35):
        hyz[4 * k : 4 * k + 4, :] = hy[k] if k < 32 else hd[k - 32]
    hyz[140:144, :] = jnp.zeros((4, 256), F32)
    hxz[...] = times(hx[...].reshape(192, 256), wf).reshape(3, 64, 256)
    hyz[...] = times(hyz[...], wf)

    def spread(cell, edge):
        inner = raw(cell)

        def pair(m):
            if m < 16:
                return inner(m)
            return (edge(0), edge(1)) if m == 16 else (None, edge(2))

        return pair

    @pl.loop(0, 4)
    def _(c):
        rows = pl.ds(pl.multiple_of(c * 16, 16), 16)

        def store(i, p, v):
            ext[i, p, 0, rows, :] = v[:, :128]
            ext[i, p, 1, rows, :] = v[:, 128:]

        lift_x(spread(lambda k: zc[k, rows, :], lambda k: hxz[k, rows, :]), store, 18)

    def put(i, p, v):
        ext[i, p, 0, 64:68, :] = v[:, :128]
        ext[i, p, 1, 64:68, :] = v[:, 128:]

    def line(k):
        return hyz[4 * k : 4 * k + 4, :]

    lift_x(spread(line, lambda k: line(k + 32)), put, 18)

    def pair(i, acc):
        for p in range(2):
            for h in range(2):
                d, s = lift_y(lambda k: ext[i, p, h, pl.ds(k, 32, stride=2), :])
                lanes = slice(h * 128, h * 128 + 128)
                c1[i, p, 0, :, lanes] = d
                c1[i, p, 1, :, lanes] = s
                if (p, h) == (0, 1):
                    acc = acc + jnp.abs(d)
                if (p, h) == (1, 0):
                    cc1[i] = s
        return acc

    acc = lax.fori_loop(0, 16, pair, jnp.zeros((32, 128), F32))
    part[...] = jnp.full(part.shape, jnp.sum(acc), F32)
    ahead[...] = cc1[0:13]
    behind[0:480, :] = cc1[1:16].reshape(480, 128)
    for k, (i, p) in enumerate(((14, 1), (15, 0), (15, 1))):
        for q in range(2):
            for h in range(2):
                at = 480 + 192 * h + 64 * k + 32 * q
                behind[at : at + 32, :] = c1[i, p, q, :, h * 128 : h * 128 + 128]
    for i in range(16):
        for p in range(2):
            ey[2 * i + p, 0:1, :] = c1[i, p, 1, 30:31, :]
            ey[2 * i + p, 1:2, :] = c1[i, p, 0, 31:32, :]
            ey[2 * i + p, 2:3, :] = c1[i, p, 1, 31:32, :]
            ey[2 * i + p, 3:4, :] = c1[i, p, 1, 31:32, :]


def pack(cc1, r2r, r2l, ey, parts, ahead, behind, part):
    total = jnp.sum(parts[...], axis=0, keepdims=True)
    part[...] = jnp.broadcast_to(total, part.shape)
    for k in range(15):
        ahead[k] = r2l[32 * k : 32 * k + 16, :]
        behind[16 * k : 16 * k + 16, :] = r2l[32 * k + 16 : 32 * k + 32, :]
    for k in range(16):
        ahead[k + 15] = cc1[k, 0:16, :]
        behind[240 + 16 * k : 256 + 16 * k, :] = cc1[k, 16:32, :]
    for k in range(13):
        ahead[k + 31] = r2r[k, 0:16, :]
        behind[496 + 16 * k : 512 + 16 * k, :] = r2r[k, 16:32, :]
    for k in range(34):
        for h in range(2):
            to = 704 + k * 4 + 136 * h
            if k < 3:
                src = 480 + 192 * h + 64 * k
                behind[to : to + 1, :] = r2l[src + 62 : src + 63, :]
                behind[to + 1 : to + 2, :] = r2l[src + 31 : src + 32, :]
                behind[to + 2 : to + 3, :] = r2l[src + 63 : src + 64, :]
                behind[to + 3 : to + 4, :] = r2l[src + 63 : src + 64, :]
            else:
                behind[to : to + 4, :] = ey[k - 3, :, h * 128 : h * 128 + 128]


def forward_rest(
    cc1, r2r, r2l, r2u, r2d, parts, c2, s2, c3, total, x2, z2, x3, z3, w2, w3
):
    depth_weights(128, w2)
    depth_weights(64, w3)
    total[...] = jnp.sum(parts[...], axis=0, keepdims=True)

    def near(k):
        if k < 15:
            return r2l[32 * k : 32 * k + 32, :]
        return cc1[k - 15] if k < 31 else r2r[k - 31]

    def put(lo, hi):
        def store(i, p, v):
            x2[i, p, lo:hi, :] = v

        return store

    lift_x(raw(lambda k: r2d[16 * k : 16 * k + 16, :]), put(0, 16), 22)
    lift_x(raw(near), put(16, 48), 22)
    lift_x(raw(lambda k: r2u[k]), put(48, 64), 22)

    def lifted(i, p):
        x2[i, p, 64:72, :] = jnp.zeros((8, 128), F32)
        return lift_y(lambda k: x2[i, p, pl.ds(k + 1, 32, stride=2), :])

    def inner(i):
        dd, ds = lifted(i + 4, 0)
        sd, ss = lifted(i + 4, 1)
        at = pl.multiple_of(640 + i * 72, 8)
        z2[pl.ds(at, 24), :] = dd[0:24]
        z2[pl.ds(at + 24, 24), :] = ds[0:24]
        z2[pl.ds(at + 48, 24), :] = sd[0:24]
        z2[pl.ds(pl.multiple_of(128 + i * 32, 32), 32), :] = ss

    pl.loop(0, 12)(inner)
    for i in (0, 1, 2, 3, 16, 17, 18, 19):
        z2[i * 32 : i * 32 + 32, :] = lifted(i, 1)[1]
    s2[...] = times(z2[0:640, :], w2).reshape(20, 32, 128)
    c2[...] = times(z2[640:1504, :], w2).reshape(12, 3, 24, 128)

    def put3(i, p, v):
        x3[i, p, :, :] = v

    lift_x(raw(lambda k: s2[k]), put3, 10)
    for i in range(8):
        for p in range(2):
            d, s = lift_y(lambda k: x3[i, p, pl.ds(k, 12, stride=2), :])
            z3[i, p, 0, 0:4, :] = jnp.zeros((4, 128), F32)
            z3[i, p, 0, 4:16, :] = d
            z3[i, p, 1, 0:4, :] = jnp.zeros((4, 128), F32)
            z3[i, p, 1, 4:16, :] = s
    u = times(z3[...].reshape(512, 128), w3)
    c3[...] = u.reshape(8, 2, 2, 16, 128)


def left_one(r2l, k):
    lo = r2l[480 + 64 * k : 544 + 64 * k, :]
    hi = r2l[672 + 64 * k : 736 + 64 * k, :]
    return jnp.concatenate([lo, hi], axis=1).reshape(2, 32, 256)


def inverse_all(
    c1, c2, s2, c3, r2l, r2d, total, wb, out,
    y3, z3, y2, z2, y1, z1, sent,
    w2, w3, *, factor
):
    depth_weights(128, w2, True)
    depth_weights(64, w3, True)
    noise = total[...] * factor
    wide = jnp.concatenate([noise, noise], axis=1)
    scale = {(0, 0): 1.0 / DD, (0, 1): 1.0, (1, 0): 1.0, (1, 1): DD}

    for i in range(8):
        for p in range(2):
            d, s = (
                shrink(c3[i, p, q], noise * (scale[p, q] * DD * DD)) for q in range(2)
            )
            if p:
                low = lax.broadcasted_iota(jnp.int32, (16, 128), 1) < 32
                s = jnp.where(low, c3[i, 1, 1], s)
            e, o = unlift_rows(d, s)
            y3[i, p, pl.ds(2, 16, stride=2), :] = e
            y3[i, p, pl.ds(3, 16, stride=2), :] = o

    def put3(k, v):
        z3[k * 24 : k * 24 + 24, :] = v

    unlift_x(lambda m, p: y3[m, p, 8:32, :], put3, 8)
    rb2 = times(z3[...], w3).reshape(12, 24, 128)

    for i in range(12):
        for p in range(2):
            d = shrink(c2[i, 2 * p], noise * (scale[p, 0] * DD))
            s = s2[i + 4, 0:24, :] if p else c2[i, 1]
            s = shrink(s, noise * (scale[p, 1] * DD))
            if p:
                low = lax.broadcasted_iota(jnp.int32, (24, 128), 1) < 64
                s = jnp.where(low, rb2[i], s)
            e, o = unlift_rows(d, s)
            y2[i, p, pl.ds(3, 24, stride=2), :] = e
            y2[i, p, pl.ds(4, 24, stride=2), :] = o

    def put2(k, v):
        z2[k * 48 : k * 48 + 48, :] = v

    unlift_x(lambda m, p: y2[m, p, 8:56, :], put2, 12)
    z2[...] = times(z2[...], w2)

    t_d = {p: wide * scale[p, 0] for p in range(2)}
    t_s = {p: wide * scale[p, 1] for p in range(2)}

    def layer(l, p, mid_d, mid_s, cell):
        lo, hi = r2d[pl.ds(704 + l * 4, 4), :], r2d[pl.ds(840 + l * 4, 4), :]
        top = jnp.concatenate([lo, hi], axis=1)
        d_top = shrink(top[1:2], t_d[p])
        s_top = shrink(top[2:3], t_s[p])
        s_over = shrink(top[0:1], t_s[p])
        d, s = shrink(mid_d, t_d[p]), shrink(mid_s, t_s[p])
        if p:
            rebuilt = z2[pl.ds(cell * 48, 40), :]
            s = jnp.concatenate([rebuilt[8:40], s[:, 128:]], axis=1)
            s_top = jnp.concatenate([rebuilt[7:8], s_top[:, 128:]], axis=1)
            s_over = jnp.concatenate([rebuilt[6:7], s_over[:, 128:]], axis=1)
        head = lax.broadcasted_iota(jnp.int32, (32, 256), 0) == 0

        def after(row, v):
            return jnp.where(head, row, pltpu.roll(v, 1, 0))

        first = after(s_top, s) + d
        e, o = unlift(after(d_top, d), first, after(s_over + d_top, first))
        for h in range(2):
            y1[l, h, pl.ds(0, 32, stride=2), :] = e[:, h * 128 : h * 128 + 128]
            y1[l, h, pl.ds(1, 32, stride=2), :] = o[:, h * 128 : h * 128 + 128]

    for k in range(3):
        mid = left_one(r2l, k)
        layer(k, 1 - k % 2, mid[0], mid[1], (k - 2) // 2 + 2)

    @pl.loop(0, 15)
    def _(i):
        layer(2 * i + 3, 0, c1[i, 0, 0], c1[i, 0, 1], None)
        layer(2 * i + 4, 1, c1[i, 1, 0], c1[i, 1, 1], i + 3)

    layer(33, 0, c1[15, 0, 0], c1[15, 0, 1], None)

    @pl.loop(0, 4)
    def _(c):
        rows = pl.ds(pl.multiple_of(c * 16, 16), 16)

        for h in range(2):

            def load(m, p):
                return y1[2 * m - 1 + p, h, rows, :]

            def put(k, v):
                z1[k, rows, h * 128 : h * 128 + 128] = v

            unlift_x(load, put, 18)

    def send(g):
        rows = pl.ds(g * 4, 4)
        return pltpu.make_async_copy(z1.at[rows], out.at[rows], sent.at[g])

    for g in range(8):
        u = times(z1[pl.ds(g * 4, 4)].reshape(256, 256), wb)
        z1[pl.ds(g * 4, 4)] = u.reshape(4, 64, 256)
        send(g).start()

    for g in range(8):
        send(g).wait()


def call(body, outs, scratch, args, mib, in_space=VMEM, out_space=VMEM, kinds=None):
    scratch = [pltpu.VMEM(s, F32) if isinstance(s, tuple) else s for s in scratch]
    return pl.pallas_call(
        body,
        out_shape=[jax.ShapeDtypeStruct(*v) for v in zip(outs, kinds or [F32] * len(outs))],
        in_specs=[in_space] * len(args),
        out_specs=[out_space] * len(outs),
        scratch_shapes=scratch,
        compiler_params=pltpu.CompilerParams(vmem_limit_bytes=mib << 20),
    )(*args)


def shared(v, axis):
    return lax.all_to_all(v, axis, 0, 0, tiled=True)


def from_ahead(v, axis):
    n = lax.axis_size(axis)
    return lax.ppermute(v, axis, [((i + 1) % n, i) for i in range(n)])


def from_behind(v, axis):
    n = lax.axis_size(axis)
    return lax.ppermute(v, axis, [(i, (i + 1) % n) for i in range(n)])


def from_corner(v):
    nx, ny = lax.axis_size("gx"), lax.axis_size("gy")
    route = [
        ((i + 1) % nx * ny + (j + 1) % ny, i * ny + j)
        for i in range(nx)
        for j in range(ny)
    ]
    return lax.ppermute(v, ("gx", "gy"), route)


def on_device(volume):
    nx, ny = lax.axis_size("gx"), lax.axis_size("gy")
    slim = [pltpu.VMEM((384, 128), BF16)] * 2
    s, q = raw(lambda k: volume[k])(0)
    mx = jnp.stack([s, q, raw(lambda k: volume[k])(1)[1]])
    md = mx[:, 0:4]
    hd = from_corner(md)
    hx = from_ahead(mx, "gx")
    hy = from_ahead(volume[:, 0:4], "gy")
    zc, wf, wb = call(
        depth_one,
        [volume.shape, (768, 256), (768, 256)],
        [],
        [volume],
        8,
        kinds=[F32, BF16, BF16],
    )
    c1, cc1, ahead, behind, part, ey = call(
        forward_one,
        [
            (16, 2, 2, 32, 256), (16, 32, 128), (13, 32, 128), (864, 128),
            (ny, 128), (32, 4, 256),
        ],
        [(16, 2, 2, 72, 128), (3, 64, 256), (144, 256)],
        [zc, hx, hy, hd, wf],
        16,
    )
    r2l = from_behind(behind, "gx")
    r2r = from_ahead(ahead, "gx")
    parts = shared(part, "gy")
    ahead, behind, part = call(
        pack, [(44, 16, 128), (976, 128), (nx, 128)], [], [cc1, r2r, r2l, ey, parts], 4
    )
    r2d = from_behind(behind, "gy")
    r2u = from_ahead(ahead, "gy")
    parts = shared(part, "gx")
    c2, s2, c3, total = call(
        forward_rest,
        [(12, 3, 24, 128), (20, 32, 128), (8, 2, 2, 16, 128), (1, 128)],
        [(20, 2, 72, 128), (1504, 128), (8, 2, 32, 128), (8, 2, 2, 16, 128), *slim],
        [cc1, r2r, r2l, r2u, r2d, parts],
        10,
    )
    count = nx * ny * volume.size // 8
    factor = math.sqrt(math.pi / 2.0) / count * DD

    def body(*refs):
        inverse_all(*refs, factor=factor)

    (out,) = call(
        body,
        [volume.shape],
        [
            (8, 2, 40, 128), (288, 128), (12, 2, 56, 128), (960, 128),
            (34, 2, 64, 128), (32, 64, 256),
            pltpu.SemaphoreType.DMA((8,)), *slim,
        ],
        [c1, c2, s2, c3, r2l, r2d, total, wb],
        16,
        out_space=HBM,
    )
    return out


def solution(mesh):
    return jax.shard_map(
        on_device,
        mesh=mesh,
        in_specs=(P("gx", "gy", None),),
        out_specs=P("gx", "gy", None),
        check_vma=False,
    )
```

```python
import math

import jax
import jax.numpy as jnp
from jax import lax
from jax.experimental import pallas as pl
from jax.experimental.pallas import tpu as pltpu
from jax.sharding import PartitionSpec as P

R3 = math.sqrt(3.0)
NEAR = R3 / 4.0
FAR = (R3 - 2.0) / 4.0
K0 = (R3 - 1.0) / math.sqrt(2.0)
K1 = (R3 + 1.0) / math.sqrt(2.0)
DD = K1 * K1
F32 = jnp.float32
BF16 = jnp.bfloat16
BLOCKS = [
    (k, q, h)
    for k in range(3)
    for q in range(2)
    for h in range(2)
    if k == 1 or q == 0 or h == 1
]
VMEM = pl.BlockSpec(memory_space=pltpu.VMEM)
HBM = pl.BlockSpec(memory_space=pltpu.HBM)


def depth_weights(n, ref, back=False):
    size = ref.shape[0] // 3
    low = {0: 1 + FAR, 1: R3 * (1 + FAR), 2: NEAR, 3: NEAR * R3 - 1}
    high = {0: -NEAR, 1: 1 - NEAR * R3, n - 2: -FAR, n - 1: -FAR * R3}
    low = {k: K0 * v for k, v in low.items()}
    high = {k: K1 * v for k, v in high.items()}

    def block(shape, row, col, kinds):
        cell = row + lax.broadcasted_iota(jnp.int32, shape, 0)
        place = col + lax.broadcasted_iota(jnp.int32, shape, 1)
        if back:
            cell, place = place, cell
        at = (cell - 2 * place) & (n - 1)
        parts = []
        for kind in kinds:
            w = jnp.zeros(shape, F32)
            for k, v in kind.items():
                w = jnp.where(at == k, v, w)
            parts.append(w)
        w = parts[0]
        if len(parts) > 1:
            w = jnp.where(place < n // 2, w, parts[1])
        if size > n:
            w = jnp.where((cell < n) & (place < n), w, 0.0)
        return w

    def save(row, col, w):
        hi = w.astype(BF16)
        lo = (w - hi.astype(F32)).astype(BF16)
        rows, cols = w.shape
        for base, v in ((0, hi), (size, hi), (2 * size, lo)):
            ref[base + row : base + row + rows, col : col + cols] = v

    if n == 256:
        for half, kind in ((0, low), (128, high)):
            shape, at = ((128, 256), (half, 0)) if back else ((256, 128), (0, half))
            save(*at, block(shape, *at, (kind,)))
    else:
        save(0, 0, block((size, size), 0, 0, (low, high)))


def times(x, w_ref):
    hi = x.astype(BF16)
    lo = (x - hi.astype(F32)).astype(BF16)
    x = jnp.concatenate([hi, lo, hi], axis=1)
    return jnp.dot(x, w_ref[...], preferred_element_type=F32)


def raw(cell):
    def pair(m):
        o = cell(2 * m + 1)
        s = cell(2 * m) + R3 * o
        return s, o - NEAR * s

    return pair


def lift_x(pair, store, pairs):
    s0, _ = pair(0)
    s1, q1 = pair(1)
    d1 = q1 - FAR * s0
    for m in range(1, pairs - 1):
        s2, q2 = pair(m + 1)
        d2 = q2 - FAR * s1
        store(m - 1, 0, d1)
        store(m - 1, 1, s1 - d2)
        s1, d1 = s2, d2


def lift_y(load):
    s0 = load(0) + R3 * load(1)
    o1 = load(3)
    s1 = load(2) + R3 * o1
    o2 = load(5)
    s2 = load(4) + R3 * o2
    d1 = o1 - NEAR * s1 - FAR * s0
    d2 = o2 - NEAR * s2 - FAR * s1
    return d1, s1 - d2


def unlift(d0, first, before):
    o = d0 + NEAR * first + FAR * before
    return first - R3 * o, o


def unlift_rows(d, s):
    first = s + pltpu.roll(d, d.shape[0] - 1, 0)
    return unlift(d, first, pltpu.roll(first, 1, 0))


def unlift_x(load, store, pairs):
    d1 = load(1, 0)
    before = load(0, 1) + d1
    for m in range(1, pairs - 1):
        d2 = load(m + 1, 0)
        first = load(m, 1) + d2
        o = d1 + NEAR * first + FAR * before
        store(2 * m - 2, first - R3 * o)
        store(2 * m - 1, o)
        d1, before = d2, first


def shrink(c, t):
    return c - jnp.clip(c, -t, t)


def depth_one(vol, zc, wf, wb):
    depth_weights(256, wf)
    depth_weights(256, wb, True)

    for g in range(4):
        rows = slice(g * 8, g * 8 + 8)
        u = times(vol[rows].reshape(512, 256), wf)
        zc[rows] = u.reshape(8, 64, 256)


def forward_one(
    zc, hx, hy, hd, wf, c1, cc1, ahead, behind, part, ey, ext, hxz, hyz
):
    for k in range(35):
        hyz[4 * k : 4 * k + 4, :] = hy[k] if k < 32 else hd[k - 32]
    hyz[140:144, :] = jnp.zeros((4, 256), F32)
    hxz[...] = times(hx[...].reshape(192, 256), wf).reshape(3, 64, 256)
    hyz[...] = times(hyz[...], wf)

    def spread(cell, edge):
        inner = raw(cell)

        def pair(m):
            if m < 16:
                return inner(m)
            return (edge(0), edge(1)) if m == 16 else (None, edge(2))

        return pair

    @pl.loop(0, 4)
    def _(c):
        rows = pl.ds(pl.multiple_of(c * 16, 16), 16)

        def store(i, p, v):
            ext[i, p, 0, rows, :] = v[:, :128]
            ext[i, p, 1, rows, :] = v[:, 128:]

        lift_x(spread(lambda k: zc[k, rows, :], lambda k: hxz[k, rows, :]), store, 18)

    def put(i, p, v):
        ext[i, p, 0, 64:68, :] = v[:, :128]
        ext[i, p, 1, 64:68, :] = v[:, 128:]

    def line(k):
        return hyz[4 * k : 4 * k + 4, :]

    lift_x(spread(line, lambda k: line(k + 32)), put, 18)

    def pair(i, acc):
        for p in range(2):
            for h in range(2):
                d, s = lift_y(lambda k: ext[i, p, h, pl.ds(k, 32, stride=2), :])
                lanes = slice(h * 128, h * 128 + 128)
                c1[i, p, 0, :, lanes] = d
                c1[i, p, 1, :, lanes] = s
                if (p, h) == (0, 1):
                    acc = acc + jnp.abs(d)
                if (p, h) == (1, 0):
                    cc1[i] = s
        return acc

    acc = lax.fori_loop(0, 16, pair, jnp.zeros((32, 128), F32))
    part[...] = jnp.full(part.shape, jnp.sum(acc), F32)
    ahead[0:11] = cc1[0:11]
    ahead[11] = raw(lambda k: cc1[11 + k])(0)[1]
    behind[0:32, :] = raw(lambda k: cc1[1 + k])(0)[0]
    behind[32:448, :] = cc1[3:16].reshape(416, 128)
    for n, (k, q, h) in enumerate(BLOCKS):
        i, p = ((14, 1), (15, 0), (15, 1))[k]
        at = 448 + 32 * n
        behind[at : at + 32, :] = c1[i, p, q, :, h * 128 : h * 128 + 128]
    for i in range(16):
        for p in range(2):
            ey[2 * i + p, 0:1, :] = c1[i, p, 1, 30:31, :]
            ey[2 * i + p, 1:2, :] = c1[i, p, 0, 31:32, :]
            ey[2 * i + p, 2:3, :] = c1[i, p, 1, 31:32, :]
            ey[2 * i + p, 3:4, :] = c1[i, p, 1, 31:32, :]


def pack(cc1, r2r, r2l, ey, parts, ahead, behind, part):
    total = jnp.sum(parts[...], axis=0, keepdims=True)
    part[...] = jnp.broadcast_to(total, part.shape)
    for k in range(14):
        ahead[k] = r2l[32 * k : 32 * k + 16, :]
        behind[16 * k : 16 * k + 16, :] = r2l[32 * k + 16 : 32 * k + 32, :]
    for k in range(16):
        ahead[k + 14] = cc1[k, 0:16, :]
        behind[224 + 16 * k : 240 + 16 * k, :] = cc1[k, 16:32, :]
    for k in range(12):
        ahead[k + 30] = r2r[k, 0:16, :]
        behind[480 + 16 * k : 496 + 16 * k, :] = r2r[k, 16:32, :]
    for k in range(34):
        for h in range(2):
            to = 672 + k * 4 + 136 * h
            if k < 3:
                s_at = 448 + 32 * BLOCKS.index((k, 1, h if k == 1 else 1))
                d_at = 448 + 32 * BLOCKS.index((k, 0, h))
                behind[to : to + 1, :] = r2l[s_at + 30 : s_at + 31, :]
                behind[to + 1 : to + 2, :] = r2l[d_at + 31 : d_at + 32, :]
                behind[to + 2 : to + 3, :] = r2l[s_at + 31 : s_at + 32, :]
                behind[to + 3 : to + 4, :] = r2l[s_at + 31 : s_at + 32, :]
            else:
                behind[to : to + 4, :] = ey[k - 3, :, h * 128 : h * 128 + 128]


def forward_rest(
    cc1, r2r, r2l, r2u, r2d, parts, c2, s2, c3, total, x2, z2, x3, z3, w2, w3
):
    depth_weights(128, w2)
    depth_weights(64, w3)
    total[...] = jnp.sum(parts[...], axis=0, keepdims=True)

    def near(k):
        if k < 14:
            return r2l[32 * k : 32 * k + 32, :]
        return cc1[k - 14] if k < 30 else r2r[k - 30]

    def edged(layer):
        inside = raw(lambda k: layer(k - 1))

        def pair(m):
            if m == 0:
                return layer(0), None
            return inside(m) if m < 21 else (None, layer(41))

        return pair

    def put(lo, hi):
        def store(i, p, v):
            x2[i, p, lo:hi, :] = v

        return store

    lift_x(edged(lambda k: r2d[16 * k : 16 * k + 16, :]), put(0, 16), 22)
    lift_x(edged(near), put(16, 48), 22)
    lift_x(edged(lambda k: r2u[k]), put(48, 64), 22)

    def lifted(i, p):
        x2[i, p, 64:72, :] = jnp.zeros((8, 128), F32)
        return lift_y(lambda k: x2[i, p, pl.ds(k + 1, 32, stride=2), :])

    def inner(i):
        dd, ds = lifted(i + 4, 0)
        sd, ss = lifted(i + 4, 1)
        at = pl.multiple_of(640 + i * 72, 8)
        z2[pl.ds(at, 24), :] = dd[0:24]
        z2[pl.ds(at + 24, 24), :] = ds[0:24]
        z2[pl.ds(at + 48, 24), :] = sd[0:24]
        z2[pl.ds(pl.multiple_of(128 + i * 32, 32), 32), :] = ss

    pl.loop(0, 12)(inner)
    for i in (0, 1, 2, 3, 16, 17, 18, 19):
        z2[i * 32 : i * 32 + 32, :] = lifted(i, 1)[1]
    s2[...] = times(z2[0:640, :], w2).reshape(20, 32, 128)
    c2[...] = times(z2[640:1504, :], w2).reshape(12, 3, 24, 128)

    def put3(i, p, v):
        x3[i, p, :, :] = v

    lift_x(raw(lambda k: s2[k]), put3, 10)
    for i in range(8):
        for p in range(2):
            d, s = lift_y(lambda k: x3[i, p, pl.ds(k, 12, stride=2), :])
            z3[i, p, 0, 0:4, :] = jnp.zeros((4, 128), F32)
            z3[i, p, 0, 4:16, :] = d
            z3[i, p, 1, 0:4, :] = jnp.zeros((4, 128), F32)
            z3[i, p, 1, 4:16, :] = s
    u = times(z3[...].reshape(512, 128), w3)
    c3[...] = u.reshape(8, 2, 2, 16, 128)


def left_one(r2l, k):
    def half(q, h):
        at = 448 + 32 * BLOCKS.index((k, q, h if (k, q, h) in BLOCKS else 1))
        return r2l[at : at + 32, :]

    return [jnp.concatenate([half(q, 0), half(q, 1)], axis=1) for q in range(2)]


def inverse_all(
    c1, c2, s2, c3, r2l, r2d, total, wb, out,
    y3, z3, y2, z2, y1, z1, sent,
    w2, w3, *, factor
):
    depth_weights(128, w2, True)
    depth_weights(64, w3, True)
    noise = total[...] * factor
    wide = jnp.concatenate([noise, noise], axis=1)
    scale = {(0, 0): 1.0 / DD, (0, 1): 1.0, (1, 0): 1.0, (1, 1): DD}

    for i in range(8):
        for p in range(2):
            d, s = (
                shrink(c3[i, p, q], noise * (scale[p, q] * DD * DD)) for q in range(2)
            )
            if p:
                low = lax.broadcasted_iota(jnp.int32, (16, 128), 1) < 32
                s = jnp.where(low, c3[i, 1, 1], s)
            e, o = unlift_rows(d, s)
            y3[i, p, pl.ds(2, 16, stride=2), :] = e
            y3[i, p, pl.ds(3, 16, stride=2), :] = o

    def put3(k, v):
        z3[k * 24 : k * 24 + 24, :] = v

    unlift_x(lambda m, p: y3[m, p, 8:32, :], put3, 8)
    rb2 = times(z3[...], w3).reshape(12, 24, 128)

    for i in range(12):
        for p in range(2):
            d = shrink(c2[i, 2 * p], noise * (scale[p, 0] * DD))
            s = s2[i + 4, 0:24, :] if p else c2[i, 1]
            s = shrink(s, noise * (scale[p, 1] * DD))
            if p:
                low = lax.broadcasted_iota(jnp.int32, (24, 128), 1) < 64
                s = jnp.where(low, rb2[i], s)
            e, o = unlift_rows(d, s)
            y2[i, p, pl.ds(3, 24, stride=2), :] = e
            y2[i, p, pl.ds(4, 24, stride=2), :] = o

    def put2(k, v):
        z2[k * 48 : k * 48 + 48, :] = v

    unlift_x(lambda m, p: y2[m, p, 8:56, :], put2, 12)
    z2[...] = times(z2[...], w2)

    t_d = {p: wide * scale[p, 0] for p in range(2)}
    t_s = {p: wide * scale[p, 1] for p in range(2)}

    def layer(l, p, mid_d, mid_s, cell):
        lo, hi = r2d[pl.ds(672 + l * 4, 4), :], r2d[pl.ds(808 + l * 4, 4), :]
        top = jnp.concatenate([lo, hi], axis=1)
        d_top = shrink(top[1:2], t_d[p])
        s_top = shrink(top[2:3], t_s[p])
        s_over = shrink(top[0:1], t_s[p])
        d, s = shrink(mid_d, t_d[p]), shrink(mid_s, t_s[p])
        if p:
            rebuilt = z2[pl.ds(cell * 48, 40), :]
            s = jnp.concatenate([rebuilt[8:40], s[:, 128:]], axis=1)
            s_top = jnp.concatenate([rebuilt[7:8], s_top[:, 128:]], axis=1)
            s_over = jnp.concatenate([rebuilt[6:7], s_over[:, 128:]], axis=1)
        head = lax.broadcasted_iota(jnp.int32, (32, 256), 0) == 0

        def after(row, v):
            return jnp.where(head, row, pltpu.roll(v, 1, 0))

        first = after(s_top, s) + d
        e, o = unlift(after(d_top, d), first, after(s_over + d_top, first))
        for h in range(2):
            y1[l, h, pl.ds(0, 32, stride=2), :] = e[:, h * 128 : h * 128 + 128]
            y1[l, h, pl.ds(1, 32, stride=2), :] = o[:, h * 128 : h * 128 + 128]

    for k in range(3):
        mid = left_one(r2l, k)
        layer(k, 1 - k % 2, mid[0], mid[1], (k - 2) // 2 + 2)

    @pl.loop(0, 15)
    def _(i):
        layer(2 * i + 3, 0, c1[i, 0, 0], c1[i, 0, 1], None)
        layer(2 * i + 4, 1, c1[i, 1, 0], c1[i, 1, 1], i + 3)

    layer(33, 0, c1[15, 0, 0], c1[15, 0, 1], None)

    def send(g):
        rows = pl.ds(g * 4, 4)
        return pltpu.make_async_copy(z1.at[rows], out.at[rows], sent.at[g])

    def ready(g):
        for c in range(2):
            for h in range(2):

                def load(m, p):
                    return y1[2 * (m + 2 * g) - 1 + p, h, c * 32 : c * 32 + 32, :]

                def put(k, v):
                    z1[4 * g + k, c * 32 : c * 32 + 32, h * 128 : h * 128 + 128] = v

                unlift_x(load, put, 4)

    for g in range(8):
        ready(g)
        u = times(z1[pl.ds(g * 4, 4)].reshape(256, 256), wb)
        z1[pl.ds(g * 4, 4)] = u.reshape(4, 64, 256)
        send(g).start()

    for g in range(8):
        send(g).wait()


def call(body, outs, scratch, args, mib, in_space=VMEM, out_space=VMEM, kinds=None):
    scratch = [pltpu.VMEM(s, F32) if isinstance(s, tuple) else s for s in scratch]
    return pl.pallas_call(
        body,
        out_shape=[jax.ShapeDtypeStruct(*v) for v in zip(outs, kinds or [F32] * len(outs))],
        in_specs=[in_space] * len(args),
        out_specs=[out_space] * len(outs),
        scratch_shapes=scratch,
        compiler_params=pltpu.CompilerParams(vmem_limit_bytes=mib << 20),
    )(*args)


def shared(v, axis):
    return lax.all_to_all(v, axis, 0, 0, tiled=True)


def from_ahead(v, axis):
    n = lax.axis_size(axis)
    return lax.ppermute(v, axis, [((i + 1) % n, i) for i in range(n)])


def from_behind(v, axis):
    n = lax.axis_size(axis)
    return lax.ppermute(v, axis, [(i, (i + 1) % n) for i in range(n)])


def from_corner(v):
    nx, ny = lax.axis_size("gx"), lax.axis_size("gy")
    route = [
        ((i + 1) % nx * ny + (j + 1) % ny, i * ny + j)
        for i in range(nx)
        for j in range(ny)
    ]
    return lax.ppermute(v, ("gx", "gy"), route)


def on_device(volume):
    nx, ny = lax.axis_size("gx"), lax.axis_size("gy")
    slim = [pltpu.VMEM((384, 128), BF16)] * 2
    s, q = raw(lambda k: volume[k])(0)
    mx = jnp.stack([s, q, raw(lambda k: volume[k])(1)[1]])
    md = mx[:, 0:4]
    hd = from_corner(md)
    hx = from_ahead(mx, "gx")
    hy = from_ahead(volume[:, 0:4], "gy")
    zc, wf, wb = call(
        depth_one,
        [volume.shape, (768, 256), (768, 256)],
        [],
        [volume],
        8,
        kinds=[F32, BF16, BF16],
    )
    c1, cc1, ahead, behind, part, ey = call(
        forward_one,
        [
            (16, 2, 2, 32, 256), (16, 32, 128), (12, 32, 128), (768, 128),
            (ny, 128), (32, 4, 256),
        ],
        [(16, 2, 2, 72, 128), (3, 64, 256), (144, 256)],
        [zc, hx, hy, hd, wf],
        16,
    )
    r2l = from_behind(behind, "gx")
    r2r = from_ahead(ahead, "gx")
    parts = shared(part, "gy")
    ahead, behind, part = call(
        pack, [(42, 16, 128), (944, 128), (nx, 128)], [], [cc1, r2r, r2l, ey, parts], 4
    )
    r2d = from_behind(behind, "gy")
    r2u = from_ahead(ahead, "gy")
    parts = shared(part, "gx")
    c2, s2, c3, total = call(
        forward_rest,
        [(12, 3, 24, 128), (20, 32, 128), (8, 2, 2, 16, 128), (1, 128)],
        [(20, 2, 72, 128), (1504, 128), (8, 2, 32, 128), (8, 2, 2, 16, 128), *slim],
        [cc1, r2r, r2l, r2u, r2d, parts],
        10,
    )
    count = nx * ny * volume.size // 8
    factor = math.sqrt(math.pi / 2.0) / count * DD

    def body(*refs):
        inverse_all(*refs, factor=factor)

    (out,) = call(
        body,
        [volume.shape],
        [
            (8, 2, 40, 128), (288, 128), (12, 2, 56, 128), (960, 128),
            (34, 2, 64, 128), (32, 64, 256),
            pltpu.SemaphoreType.DMA((8,)), *slim,
        ],
        [c1, c2, s2, c3, r2l, r2d, total, wb],
        16,
        out_space=HBM,
    )
    return out


def solution(mesh):
    return jax.shard_map(
        on_device,
        mesh=mesh,
        in_specs=(P("gx", "gy", None),),
        out_specs=P("gx", "gy", None),
        check_vma=False,
    )
```
